32 devices in a mesh: dp: 4 (over x, core), expert: 8 (over z, y).
Axes of the slice: x: 2, y: 2, z: 4, core: 2. Of those that a mesh axis runs over, the one named last changes fastest.
Arguments:
- tokens: bfloat16 [4096, 2048], P(('dp', 'expert')), may hold values from -6 to 6
- expert_ids: int32 [4096, 4], P(('dp', 'expert')), may hold values from 0 to 15, all different within a row; in each aligned block of 128 rows (0 to 127, 128 to 255, ...) at most 48 rows name the same one
- gate_weights: float32 [4096, 4], P(('dp', 'expert')), may hold values from 0.05 to 0.6
- grad_out: bfloat16 [4096, 2048], P(('dp', 'expert')), may hold values from -6 to 6
- w_gate: bfloat16 [16, 2048, 384], P('expert'), may hold values from -0.125 to 0.125
- w_up: bfloat16 [16, 2048, 384], P('expert'), may hold values from -0.125 to 0.125
- w_down: bfloat16 [16, 384, 2048], P('expert'), may hold values from -0.3125 to 0.3125
Outputs:
- mixed_out: bfloat16 [4096, 2048], P(('dp', 'expert'))
- d_tokens: bfloat16 [4096, 2048], P(('dp', 'expert'))
- d_gates: float32 [4096, 4], P(('dp', 'expert'))
- d_w_gate: bfloat16 [16, 2048, 384], P('expert', 'dp')
- d_w_up: bfloat16 [16, 2048, 384], P('expert', 'dp')
- d_w_down: bfloat16 [16, 384, 2048], P('expert', None, 'dp')
The draws below stay inside these ranges and needn't reach their ends.
Inputs may be any that keep to these rules, and one draw needn't show every extreme that they name: `expert_ids`: each row names 4 different experts; in the 128 rows of one device no expert is named more than 48 times, and in every draw some expert is named exactly 48 times by the rows of some device.
All inputs are finite; a program needn't handle non-finite values.
Results may differ from the reference program's by a relative error of at most 0.009.
Values may be sent and summed in bfloat16 or wider, within the bound.
A program may use at most 128 MiB of HBM per device.

```python
import math
import jax
import jax.numpy as jnp
import numpy as np
from jax import lax

D = 2048
FF = 384
TOP = 4
TOK_DEV = 128
EXPERTS = 16
CAP = 48
TOKENS = 4096
N_DP = 4
N_EXPERT = 8


def shard_levels(stream_key, shape, pieces, low, top_value):
    def one(dim, shards_of):
        draws = jax.random.uniform(jax.random.fold_in(jax.random.fold_in(stream_key, 6), dim), (shards_of,), jnp.float32, low / len(pieces), top_value / len(pieces))
        return jnp.repeat(jnp.exp(draws), shape[dim] // shards_of).reshape((-1,) + (1,) * (len(shape) - dim - 1))

    factor_of = one(*pieces[0])
    for cut in pieces[1:]:
        factor_of = factor_of * one(*cut)
    return factor_of


def deal_out(rng, own, number, rows, number_of, top, limit, skew):
    order = jax.random.permutation(rng, number_of)
    packed, usual = shares(number_of, rows * top, limit, skew, True), shares(number_of, rows * top, limit, skew, False)
    places = jnp.arange(number_of)

    def named(tallies, rotation):
        used = int((tallies > 0).sum())
        fixed = max(1, used // 4)
        shifted = fixed + (places - fixed + rotation * (used - fixed)) % max(1, number_of - fixed)
        return jnp.zeros((number_of,), jnp.int32).at[order[jnp.where(places < fixed, places, shifted)]].set(jnp.asarray(tallies, jnp.int32))

    tallies = jnp.where(number % 4 == 0, named(packed, number // 4), named(usual, number - number // 4 - 1))
    mixed = jax.random.permutation(jax.random.fold_in(own, 3), number_of)
    donor, taker = mixed[0:number_of // 2 * 2:2], mixed[1:number_of // 2 * 2:2]
    slack = jnp.minimum(tallies[donor] - 1, limit - tallies[taker]) // 2
    slack = jnp.where((donor == order[0]) | (taker == order[0]) | (tallies[taker] == 0), 0, jnp.maximum(slack, 0))
    shifted = jax.random.randint(jax.random.fold_in(own, 4), (number_of // 2,), 0, 1 << 20) % (slack + 1)
    tallies = tallies.at[donor].add(-shifted).at[taker].add(shifted)
    members = jnp.searchsorted(jnp.cumsum(tallies), jnp.arange(rows * top), side="right").astype(jnp.int32)
    grid = members.reshape(top, rows).T
    grid = grid[jax.random.permutation(jax.random.fold_in(own, 1), rows)]
    rotation = jax.random.randint(jax.random.fold_in(own, 2), (rows, 1), 0, top)
    return jnp.take_along_axis(grid, (jnp.arange(top)[None, :] + rotation) % top, axis=1)


def shares(number_of, total, most, skew, full):
    weights = [(1 << 20) // math.isqrt(rank ** skew) + 1 for rank in range(1, number_of + 1)]
    largest = most if full else min(most, max(-(-total // number_of), total * weights[0] // sum(weights)))
    least = 1 if total - largest >= number_of - 1 else 0
    holding, rest = [largest] + [least] * (number_of - 1), total - largest - least * (number_of - 1)
    while rest > 0:
        free = [i for i in range(1, number_of) if holding[i] < largest] or [i for i in range(1, number_of) if holding[i] < most]
        mass, budget = sum([weights[i] for i in free]), rest
        for i in free:
            extra = min(most - holding[i], max(1, budget * weights[i] // mass), rest)
            holding[i] = holding[i] + extra
            rest = rest - extra
    return np.array(holding)


def gaussian(rng, extent, deviation, reach, pieces=(), held_as=jnp.bfloat16):
    entries = deviation * jax.random.normal(rng, extent, jnp.float32)
    if pieces:
        entries = entries * shard_levels(rng, extent, pieces, -0.22, 0.18)
    return jnp.clip(entries, -reach, reach).astype(held_as)


def setup_inputs(seed: int = 0) -> dict:
    arg_keys = jax.random.split(jax.random.key(seed), 8)
    tokens = gaussian(arg_keys[0], (TOKENS, D), 1.0, 6.0, ((0, 32),))
    expert_ids_keys = jax.random.split(jax.random.fold_in(arg_keys[1], 1), TOKENS // TOK_DEV)
    expert_ids_turns = jax.random.permutation(jax.random.fold_in(arg_keys[1], 3), TOKENS // TOK_DEV)
    expert_ids = jax.vmap(lambda own, number: deal_out(jax.random.fold_in(arg_keys[1], 2), own, number, TOK_DEV, EXPERTS, TOP, CAP, 2))(expert_ids_keys, expert_ids_turns).reshape((TOKENS, TOP))
    gate_weights = jnp.clip(0.05 + 0.55 * jax.random.uniform(arg_keys[2], (TOKENS, TOP), jnp.float32) ** shard_levels(arg_keys[2], (TOKENS, TOP), ((0, 32),), -0.2, 0.2), 0.05, 0.6)
    grad_out = gaussian(arg_keys[3], (TOKENS, D), 1.0, 6.0, ((0, 32),))
    w_gate = gaussian(arg_keys[4], (EXPERTS, D, FF), D ** -0.5, 0.125, ((0, 8),))
    w_up = gaussian(arg_keys[5], (EXPERTS, D, FF), D ** -0.5, 0.125, ((0, 8),))
    w_down = gaussian(arg_keys[6], (EXPERTS, FF, D), FF ** -0.5, 0.3125, ((0, 8),))
    return dict(tokens=tokens, expert_ids=expert_ids, gate_weights=gate_weights, grad_out=grad_out, w_gate=w_gate, w_up=w_up, w_down=w_down)


def summed_groups(partials):
    rounded = partials.astype(jnp.bfloat16)
    rounded = lax.optimization_barrier(rounded)
    return jnp.sum(rounded.astype(jnp.float32), axis=0).astype(jnp.bfloat16)


def reference(tokens, expert_ids, gate_weights, grad_out, w_gate, w_up, w_down):
    device_count = N_DP * N_EXPERT
    routes_dev = TOK_DEV * TOP
    slot_count = device_count * CAP
    route_total = TOKENS * TOP
    ids_dev = expert_ids.reshape(device_count, routes_dev).astype(jnp.int32)
    onehot = (ids_dev[:, :, None] == jnp.arange(EXPERTS, dtype=jnp.int32)[None, None, :]).astype(jnp.int32)
    earlier = jnp.cumsum(onehot, axis=1) - onehot
    slot_pos = jnp.sum(earlier * onehot, axis=2).astype(jnp.int32)
    device_ids = jnp.arange(device_count, dtype=jnp.int32)[:, None]
    position = (ids_dev * slot_count + device_ids * CAP + slot_pos).reshape(-1).astype(jnp.int32)
    route_of = jnp.full((EXPERTS * slot_count,), route_total, dtype=jnp.int32)
    route_of = route_of.at[position].set(jnp.arange(route_total, dtype=jnp.int32)).reshape(EXPERTS, slot_count)
    tokens_ext = jnp.concatenate([tokens, jnp.zeros((1, D), tokens.dtype)], axis=0)
    grad_ext = jnp.concatenate([grad_out, jnp.zeros((1, D), grad_out.dtype)], axis=0)
    gates_ext = jnp.concatenate([gate_weights.reshape(-1), jnp.zeros((1,), gate_weights.dtype)], axis=0)

    def per_expert(totals, inputs):
        out_acc, dx_acc, dgate_acc = totals
        routes_e, gate_w, up_w, down_w = inputs
        token_e = routes_e // TOP
        slot_rows = tokens_ext[token_e]
        gate_pre = jnp.dot(slot_rows, gate_w, preferred_element_type=jnp.float32)
        up_pre = jnp.dot(slot_rows, up_w, preferred_element_type=jnp.float32)
        hidden = (jax.nn.silu(gate_pre) * up_pre).astype(jnp.bfloat16)
        expert_out = jnp.dot(hidden, down_w, preferred_element_type=jnp.float32).astype(jnp.bfloat16)
        weight_e = gates_ext[routes_e].astype(jnp.float32)
        out_f = expert_out.astype(jnp.float32)
        out_acc = out_acc.at[token_e].add(weight_e[:, None] * out_f)
        grad_rows = grad_ext[token_e].astype(jnp.float32)
        dgate_acc = dgate_acc.at[routes_e].add(jnp.sum(out_f * grad_rows, axis=1))
        scaled = (weight_e[:, None] * grad_rows).astype(jnp.bfloat16)
        d_hidden = jnp.dot(scaled, down_w.T, preferred_element_type=jnp.float32)
        sigma_gate = jax.nn.sigmoid(gate_pre)
        d_up = (d_hidden * gate_pre * sigma_gate).astype(jnp.bfloat16)
        d_gate = (d_hidden * up_pre * sigma_gate * (1.0 + gate_pre * (1.0 - sigma_gate))).astype(jnp.bfloat16)
        d_rows = (jnp.dot(d_gate, gate_w.T, preferred_element_type=jnp.float32)
                  + jnp.dot(d_up, up_w.T, preferred_element_type=jnp.float32)).astype(jnp.bfloat16)
        dx_acc = dx_acc.at[token_e].add(d_rows.astype(jnp.float32))
        group_rows = slot_rows.astype(jnp.float32).reshape(N_DP, N_EXPERT * CAP, D)
        group_scaled = scaled.astype(jnp.float32).reshape(N_DP, N_EXPERT * CAP, D)
        group_gate = d_gate.astype(jnp.float32).reshape(N_DP, N_EXPERT * CAP, FF)
        group_up = d_up.astype(jnp.float32).reshape(N_DP, N_EXPERT * CAP, FF)
        group_hidden = hidden.astype(jnp.float32).reshape(N_DP, N_EXPERT * CAP, FF)
        grad_gate = summed_groups(jnp.einsum("gsd,gsf->gdf", group_rows, group_gate))
        grad_up = summed_groups(jnp.einsum("gsd,gsf->gdf", group_rows, group_up))
        grad_down = summed_groups(jnp.einsum("gsf,gsd->gfd", group_hidden, group_scaled))
        return (out_acc, dx_acc, dgate_acc), (grad_gate, grad_up, grad_down)

    start = (jnp.zeros((TOKENS + 1, D), jnp.float32), jnp.zeros((TOKENS + 1, D), jnp.float32),
             jnp.zeros((route_total + 1,), jnp.float32))
    totals, grads = lax.scan(per_expert, start, (route_of, w_gate, w_up, w_down))
    out_acc, dx_acc, dgate_acc = totals
    mixed_out = out_acc[:TOKENS].astype(jnp.bfloat16)
    d_tokens = dx_acc[:TOKENS].astype(jnp.bfloat16)
    d_gates = dgate_acc[:route_total].reshape(TOKENS, TOP)
    return (mixed_out, d_tokens, d_gates, grads[0], grads[1], grads[2])
```

```python
import jax
import jax.numpy as jnp
from jax import lax
from jax.sharding import PartitionSpec as P

BF16 = jnp.bfloat16
F32 = jnp.float32


def dot(spec, a, b):
    return jnp.einsum(spec, a, b, preferred_element_type=F32)


def local(tokens, expert_ids, gate_weights, grad_out, w_gate, w_up, w_down):
    tok_dev, model_dim = tokens.shape
    exp_dev = w_gate.shape[0]
    owners = lax.axis_size("expert")
    experts = exp_dev * owners
    me = lax.axis_index("expert")
    chosen = expert_ids[:, :, None] == jnp.arange(experts, dtype=jnp.int32)
    gate_of = jnp.sum(jnp.where(chosen, gate_weights[:, :, None], 0.0), axis=1)
    gates = lax.all_to_all(
        gate_of.reshape(tok_dev, owners, exp_dev).transpose(1, 2, 0), "expert", 0, 0, tiled=True
    )
    gates = gates.transpose(1, 0, 2).reshape(exp_dev, owners * tok_dev, 1)
    rows = lax.all_gather(tokens, "expert", axis=0, tiled=True)
    grads = lax.all_gather(grad_out, "expert", axis=0, tiled=True)
    gate_pre = dot("td,edf->etf", rows, w_gate)
    up_pre = dot("td,edf->etf", rows, w_up)
    d_mid = dot("td,efd->etf", grads, w_down)
    sigma = jax.nn.sigmoid(gate_pre)
    hidden = gate_pre * sigma * up_pre
    d_gate_sum = jnp.sum(hidden * d_mid, axis=2)
    d_hidden = gates * d_mid
    scaled_hidden = (gates * hidden).astype(BF16)
    d_up = (d_hidden * gate_pre * sigma).astype(BF16)
    d_gate = (d_hidden * up_pre * sigma * (1.0 + gate_pre * (1.0 - sigma))).astype(BF16)
    mixed = dot("etf,efd->td", scaled_hidden, w_down).astype(BF16)
    mixed_out = lax.psum_scatter(mixed, "expert", scatter_dimension=0, tiled=True)
    d_rows = (dot("etf,edf->td", d_gate, w_gate) + dot("etf,edf->td", d_up, w_up)).astype(BF16)
    d_tokens = lax.psum_scatter(d_rows, "expert", scatter_dimension=0, tiled=True)
    back = lax.all_to_all(
        d_gate_sum.reshape(exp_dev, owners, tok_dev).transpose(1, 0, 2), "expert", 0, 0, tiled=True
    )
    back = back.reshape(experts, tok_dev).T
    d_gates = jnp.sum(jnp.where(chosen, back[:, None, :], 0.0), axis=2)
    part_gate = dot("td,etf->edf", rows, d_gate).astype(BF16)
    part_up = dot("td,etf->edf", rows, d_up).astype(BF16)
    part_down = dot("etf,td->efd", scaled_hidden, grads).astype(BF16)
    grad_gate = lax.psum_scatter(part_gate, "dp", scatter_dimension=1, tiled=True)
    grad_up = lax.psum_scatter(part_up, "dp", scatter_dimension=1, tiled=True)
    grad_down = lax.psum_scatter(part_down, "dp", scatter_dimension=2, tiled=True)
    return (mixed_out, d_tokens, d_gates, grad_gate, grad_up, grad_down)


def solution(mesh):
    in_specs = (
        P(("dp", "expert"), None),
        P(("dp", "expert"), None),
        P(("dp", "expert"), None),
        P(("dp", "expert"), None),
        P("expert", None, None),
        P("expert", None, None),
        P("expert", None, None),
    )
    out_specs = (
        P(("dp", "expert"), None),
        P(("dp", "expert"), None),
        P(("dp", "expert"), None),
        P("expert", "dp", None),
        P("expert", "dp", None),
        P("expert", None, "dp"),
    )
    return jax.shard_map(local, mesh=mesh, in_specs=in_specs, out_specs=out_specs, check_vma=False)
```

```python
import jax
import jax.numpy as jnp
from jax import lax
from jax.sharding import PartitionSpec as P

BF16 = jnp.bfloat16
F32 = jnp.float32


def dot(spec, a, b):
    return jnp.einsum(spec, a, b, preferred_element_type=F32)


def ring_order(count):
    return list(range(0, count, 2)) + list(range(count - 1, 0, -2))


def mover(count):
    order = ring_order(count)
    right = [(order[i], order[(i + 1) % count]) for i in range(count)]
    left = [(b, a) for a, b in right]
    return (
        lambda v: lax.ppermute(v, "expert", right),
        lambda v: lax.ppermute(v, "expert", left),
    )


def gather_steps(own, rights, lefts, go_right, go_left, beside=None):
    held = {0: own}
    by_right = by_left = own
    for step in range(1, max(rights, lefts) + 1):
        if step <= rights:
            by_right = go_right(by_right)
            held[step] = by_right
        if step <= lefts:
            by_left = go_left(by_left)
            held[-step] = by_left
        if step == 2 and beside is not None:
            by_right, beside = lax.optimization_barrier((by_right, beside))
            held[step] = by_right
    return held, beside


def add(a, b):
    return (a.astype(F32) + b.astype(F32)).astype(BF16)


def return_steps(parts, rights, lefts, go_right, go_left, beside=None):
    by_left = parts[rights]
    by_right = parts[-lefts]
    for step in range(1, max(rights, lefts) + 1):
        if step <= rights:
            by_left = go_left(by_left)
            if step < rights:
                by_left = add(by_left, parts[rights - step])
        if step <= lefts:
            by_right = go_right(by_right)
            if step < lefts:
                by_right = add(by_right, parts[step - lefts])
        if beside is not None and step in beside:
            by_left, beside[step] = lax.optimization_barrier((by_left, beside[step]))
    total = parts[0].astype(F32) + by_left.astype(F32) + by_right.astype(F32)
    return total.astype(BF16), beside


def dp_sum(part, axis, dps):
    lanes = dps // 2
    size = part.shape[axis] // dps
    me = lax.axis_index("dp")
    core = me % 2
    x = me // 2
    piece = lambda i: lax.dynamic_slice_in_dim(part, i * size, size, axis)
    swap = [(i, i ^ 1) for i in range(dps)]
    far = [(x + shift) % lanes for shift in range(1, lanes)] + [x]
    sent = jnp.stack([piece(f * 2 + 1 - core) for f in far])
    got = lax.ppermute(sent, "dp", swap)
    total = None
    for i, f in enumerate(far):
        both = piece(f * 2 + core).astype(F32) + got[i].astype(F32)
        if i < lanes - 1:
            shift = i + 1
            pairs = [(d, ((d // 2 + shift) % lanes) * 2 + d % 2) for d in range(dps)]
            both = lax.ppermute(both.astype(BF16), "dp", pairs).astype(F32)
        total = both if total is None else total + both
    return total.astype(BF16)


def local_wide(tokens, expert_ids, gate_weights, grad_out, w_gate, w_up, w_down):
    tok_dev, model_dim = tokens.shape
    exp_dev = w_gate.shape[0]
    owners = lax.axis_size("expert")
    experts = exp_dev * owners
    chosen = expert_ids[:, :, None] == jnp.arange(experts, dtype=jnp.int32)
    gate_of = jnp.sum(jnp.where(chosen, gate_weights[:, :, None], 0.0), axis=1)
    gates = lax.all_to_all(
        gate_of.reshape(tok_dev, owners, exp_dev).transpose(1, 2, 0), "expert", 0, 0, tiled=True
    )
    gates = gates.transpose(1, 0, 2).reshape(exp_dev, owners * tok_dev, 1)
    rows = lax.all_gather(tokens, "expert", axis=0, tiled=True)
    grads = lax.all_gather(grad_out, "expert", axis=0, tiled=True)
    gate_pre = dot("td,edf->etf", rows, w_gate)
    up_pre = dot("td,edf->etf", rows, w_up)
    d_mid = dot("td,efd->etf", grads, w_down)
    sigma = jax.nn.sigmoid(gate_pre)
    hidden = gate_pre * sigma * up_pre
    d_gate_sum = jnp.sum(hidden * d_mid, axis=2)
    d_hidden = gates * d_mid
    scaled_hidden = (gates * hidden).astype(BF16)
    d_up = (d_hidden * gate_pre * sigma).astype(BF16)
    d_gate = (d_hidden * up_pre * sigma * (1.0 + gate_pre * (1.0 - sigma))).astype(BF16)
    mixed = dot("etf,efd->td", scaled_hidden, w_down).astype(BF16)
    mixed_out = lax.psum_scatter(mixed, "expert", scatter_dimension=0, tiled=True)
    d_rows = (dot("etf,edf->td", d_gate, w_gate) + dot("etf,edf->td", d_up, w_up)).astype(BF16)
    d_tokens = lax.psum_scatter(d_rows, "expert", scatter_dimension=0, tiled=True)
    back = lax.all_to_all(
        d_gate_sum.reshape(exp_dev, owners, tok_dev).transpose(1, 0, 2), "expert", 0, 0, tiled=True
    )
    back = back.reshape(experts, tok_dev).T
    d_gates = jnp.sum(jnp.where(chosen, back[:, None, :], 0.0), axis=2)
    part_gate = dot("td,etf->edf", rows, d_gate).astype(BF16)
    part_up = dot("td,etf->edf", rows, d_up).astype(BF16)
    part_down = dot("etf,td->efd", scaled_hidden, grads).astype(BF16)
    grad_gate = lax.psum_scatter(part_gate, "dp", scatter_dimension=1, tiled=True)
    grad_up = lax.psum_scatter(part_up, "dp", scatter_dimension=1, tiled=True)
    grad_down = lax.psum_scatter(part_down, "dp", scatter_dimension=2, tiled=True)
    return (mixed_out, d_tokens, d_gates, grad_gate, grad_up, grad_down)


def local(tokens, expert_ids, gate_weights, grad_out, w_gate, w_up, w_down):
    if lax.axis_size("expert") > 8:
        return local_wide(tokens, expert_ids, gate_weights, grad_out, w_gate, w_up, w_down)
    tok_dev, model_dim = tokens.shape
    exp_dev = w_gate.shape[0]
    owners = lax.axis_size("expert")
    dps = lax.axis_size("dp")
    experts = exp_dev * owners
    half = owners // 2
    me = lax.axis_index("expert")
    go_right, go_left = mover(owners)

    chosen = expert_ids[:, :, None] == jnp.arange(experts, dtype=jnp.int32)
    gate_of = jnp.sum(jnp.where(chosen, gate_weights[:, :, None], 0.0), axis=1)
    gates = lax.all_to_all(
        gate_of.reshape(tok_dev, owners, exp_dev).transpose(1, 2, 0), "expert", 0, 0, tiled=True
    )

    xs, gates = gather_steps(tokens, half, half - 1, go_right, go_left, gates)
    gs, _ = gather_steps(grad_out, half - 1, half, go_right, go_left)
    gs[half] = gs[-half]
    groups = []
    for lo, hi in ((0, half // 2), (half // 2 + 1, half)):
        group = []
        for step in range(lo, hi + 1):
            group += [0] if step == 0 else [half] if step == half else [step, -step]
        groups.append(group)

    position = jnp.where(me % 2 == 0, me // 2, owners - 1 - me // 2)
    order = jnp.asarray(ring_order(owners), jnp.int32)

    parts_mixed, parts_rows, parts_dots = {}, {}, {}
    kept = []
    for number, group in enumerate(groups):
        x = jnp.concatenate([xs[k] for k in group], axis=0)
        g = jnp.concatenate([gs[k] for k in group], axis=0)
        if number == 0 and half > 3:
            ahead = ([xs[3], xs[-3]], [gs[3], gs[-3]])
            g, ahead = lax.optimization_barrier((g, ahead))
            (xs[3], xs[-3]), (gs[3], gs[-3]) = ahead
        sources = order[(position - jnp.asarray(group, jnp.int32)) % owners]
        gate = gates[sources].transpose(0, 2, 1).reshape(len(group) * tok_dev, exp_dev)
        row_gate, row_up, row_mid = [], [], []
        for e in range(exp_dev):
            weight = gate[:, e : e + 1]
            gate_pre = dot("td,df->tf", x, w_gate[e])
            up_pre = dot("td,df->tf", x, w_up[e])
            d_mid = dot("td,fd->tf", g, w_down[e])
            sigma = jax.nn.sigmoid(gate_pre)
            hidden = gate_pre * sigma * up_pre
            dots = jnp.sum(hidden * d_mid, axis=1)
            d_hidden = weight * d_mid
            row_mid.append((weight * hidden).astype(BF16))
            row_up.append((d_hidden * gate_pre * sigma).astype(BF16))
            row_gate.append(
                (d_hidden * up_pre * sigma * (1.0 + gate_pre * (1.0 - sigma))).astype(BF16)
            )
            for i, k in enumerate(group):
                parts_dots[k, e] = dots[i * tok_dev : (i + 1) * tok_dev]
        d_gate = jnp.stack(row_gate)
        d_up = jnp.stack(row_up)
        mid = jnp.stack(row_mid)
        mixed = dot("etf,efd->td", mid, w_down).astype(BF16)
        rows = (dot("etf,edf->td", d_gate, w_gate) + dot("etf,edf->td", d_up, w_up)).astype(BF16)
        for i, k in enumerate(group):
            parts_mixed[k] = mixed[i * tok_dev : (i + 1) * tok_dev]
            parts_rows[k] = rows[i * tok_dev : (i + 1) * tok_dev]
        kept.append((x, g, d_gate, d_up, mid))

    all_keys = [k for group in groups for k in group]
    dots = jnp.stack([jnp.stack([parts_dots[k, e] for e in range(exp_dev)]) for k in all_keys])
    slots = [0] * owners
    for i, k in enumerate(all_keys):
        slots[k % owners] = i
    steps = (position - jnp.asarray([ring_order(owners).index(d) for d in range(owners)])) % owners
    dots = dots[jnp.asarray(slots, jnp.int32)[steps]]
    last = kept[-1]
    (parts_mixed[half], parts_rows[half]), last = lax.optimization_barrier(
        ((parts_mixed[half], parts_rows[half]), last)
    )
    kept[-1] = last
    parts_mixed[-half] = parts_mixed[half]
    parts_rows[-half] = parts_rows[half]
    back = lax.all_to_all(dots, "expert", 0, 0, tiled=True)
    x = jnp.concatenate([v[0] for v in kept], axis=0)
    g = jnp.concatenate([v[1] for v in kept], axis=0)
    d_gate, d_up, mid = (jnp.concatenate([v[i] for v in kept], axis=1) for i in (2, 3, 4))
    grad_gate = dp_sum(dot("td,etf->edf", x, d_gate).astype(BF16), 1, dps)
    grad_up = dp_sum(dot("td,etf->edf", x, d_up).astype(BF16), 1, dps)
    grad_down = dp_sum(dot("etf,td->efd", mid, g).astype(BF16), 2, dps)
    mixed_out, beside = return_steps(
        parts_mixed, half, half - 1, go_right, go_left, {2: (back, grad_gate), 3: grad_up}
    )
    if half > 3:
        (back, grad_gate), grad_up = beside[2], beside[3]
    d_tokens, _ = return_steps(parts_rows, half - 1, half, go_right, go_left)
    back = back.reshape(experts, tok_dev).T
    d_gates = jnp.sum(jnp.where(chosen, back[:, None, :], 0.0), axis=2)
    return (mixed_out, d_tokens, d_gates, grad_gate, grad_up, grad_down)


def solution(mesh):
    in_specs = (
        P(("dp", "expert"), None),
        P(("dp", "expert"), None),
        P(("dp", "expert"), None),
        P(("dp", "expert"), None),
        P("expert", None, None),
        P("expert", None, None),
        P("expert", None, None),
    )
    out_specs = (
        P(("dp", "expert"), None),
        P(("dp", "expert"), None),
        P(("dp", "expert"), None),
        P("expert", "dp", None),
        P("expert", "dp", None),
        P("expert", None, "dp"),
    )
    return jax.shard_map(local, mesh=mesh, in_specs=in_specs, out_specs=out_specs, check_vma=False)
```
